128 devices in a mesh: grp: 8 (over x, core), tp: 16 (over y, z).
Axes of the slice: x: 4, y: 4, z: 4, core: 2. Of those that a mesh axis runs over, the one named last changes fastest.
Arguments:
- layer_input: bfloat16 [8192, 2880], P(('grp', 'tp')), may hold values from -40 to 40
- attn_gain: float32 [2880], replicated, may hold values from 0.1 to 1.9
- query_weight: bfloat16 [2880, 4096], P(None, 'tp'), may hold values from -0.109375 to 0.109375
- keyval_weight: bfloat16 [2880, 1024], replicated, may hold values from -0.25 to 0.25
- output_weight: bfloat16 [4096, 2880], P('tp'), may hold values from -0.125 to 0.125
- cache_entries: bfloat16 [8, 16, 2048, 128], P('grp', 'tp'), may hold values from -500 to 500
- cache_length: int32 [8], P('grp'), may hold values from 256 to 4096, as said below
- expert_gain: float32 [2880], replicated, may hold values from 0.1 to 1.9
- router_weight: bfloat16 [2880, 32], replicated, may hold values from -30 to 30
- expert_choice: int32 [8192, 4], P(('grp', 'tp')), may hold values from 0 to 31, all different within a row; in each aligned block of 64 rows (0 to 63, 64 to 127, ...) at most 12 rows name the same one
- gate_weight: bfloat16 [128, 2880, 720], P(('grp', 'tp')), may hold values from -0.109375 to 0.109375
- up_weight: bfloat16 [128, 2880, 720], P(('grp', 'tp')), may hold values from -0.109375 to 0.109375
- down_weight: bfloat16 [128, 720, 2880], P(('grp', 'tp')), may hold values from -0.109375 to 0.109375
Outputs:
- layer_output: bfloat16 [8192, 2880], P(('grp', 'tp'))
The draws below stay inside these ranges and needn't reach their ends.
Inputs may be any that keep to these rules, and one draw needn't show every extreme that they name: `expert_choice`: each row names 4 different experts; in each aligned block of the rows of one device no expert is named by more than 12 rows. `cache_length`: one group's cache holds exactly 4096 valid keys.
All inputs are finite; a program needn't handle non-finite values.
Results may differ from the reference program's by a relative error of at most 0.039.
Values may be sent and summed in bfloat16 or wider, within the bound.
A program may use at most 128 MiB of HBM per device.

```python
import math
import jax
import jax.numpy as jnp
import numpy as np
from jax import lax

D = 2880
QH = 64
KVH = 8
HD = 64
E = 32
TOPK = 4
FF = 2880
ROWS = 1024
CTX = 4096
CSPLIT = 2
CAP = 12
FSPLIT = 4
HBLOCK = 720
TOKENS = 8192
N_GRP = 8
N_TP = 16


def draw_layer_input(key, part):
    subkeys = jax.random.split(key, 3)
    row_scale = jnp.exp(jax.random.uniform(subkeys[0], (TOKENS, 1), jnp.float32, math.log(0.3), math.log(3.0)))
    col_scale = jnp.exp(jax.random.uniform(subkeys[1], (1, D), jnp.float32, math.log(0.3), math.log(3.0)))
    entries_raw = jax.random.normal(subkeys[2], (TOKENS, D), jnp.float32)
    return jnp.clip(entries_raw * row_scale * col_scale, -40.0, 40.0).astype(jnp.bfloat16)


def draw_cache_entries(key, part):
    subkeys = jax.random.split(key, 2)
    shape_all = (N_GRP, KVH, CTX, HD)
    keys_part = 2.5 * jax.random.normal(subkeys[0], shape_all, jnp.float32)
    values_part = 2.5 * jax.random.normal(subkeys[1], shape_all, jnp.float32)
    joined = jnp.clip(jnp.concatenate([keys_part, values_part], axis=-1), -500.0, 500.0)
    return joined.reshape(N_GRP, KVH * CSPLIT, CTX // CSPLIT, 2 * HD).astype(jnp.bfloat16)


def draw_cache_length(key, part):
    subkeys = jax.random.split(key, 2)
    lengths = jax.random.randint(subkeys[0], (N_GRP,), CTX // 16, CTX + 1)
    longest = jax.random.randint(subkeys[1], (), 0, N_GRP)
    return jnp.where(jnp.arange(N_GRP) == longest, CTX, lengths).astype(jnp.int32)


def draw_router_weight(key, part):
    subkeys = jax.random.split(key, 1)
    raw_weight = jax.random.normal(subkeys[0], (D, E), jnp.float32) * D ** (-0.5)
    return jnp.clip(raw_weight, -30.0, 30.0).astype(jnp.bfloat16)


def block_scale(key, extent, shards, least, high):
    level, own = 1.0, jax.random.fold_in(key, 6)
    for position, shards_of in shards:
        steps = jnp.exp(jax.random.uniform(jax.random.fold_in(own, position), (shards_of,), jnp.float32, least / len(shards), high / len(shards)))
        level = level * jnp.repeat(steps, extent[position] // shards_of).reshape([-1 if axis == position else 1 for axis in range(len(extent))])
    return level


def shared_out(key, own, number, rows, count, top, limit, lean):
    ranking = jax.random.permutation(key, count)
    heavy_load, ordinary = portions_of(count, rows * top, limit, lean, True), portions_of(count, rows * top, limit, lean, False)
    places = jnp.arange(count)

    def named(sizes, offset_by):
        used = int((sizes > 0).sum())
        fixed = max(1, used // 4)
        passed = fixed + (places - fixed + offset_by * (used - fixed)) % max(1, count - fixed)
        return jnp.zeros((count,), jnp.int32).at[ranking[jnp.where(places < fixed, places, passed)]].set(jnp.asarray(sizes, jnp.int32))

    sizes = jnp.where(number % 4 == 0, named(heavy_load, number // 4), named(ordinary, number - number // 4 - 1))
    mixed = jax.random.permutation(jax.random.fold_in(own, 3), count)
    source_of, sink = mixed[0:count // 2 * 2:2], mixed[1:count // 2 * 2:2]
    margin = jnp.minimum(sizes[source_of] - 1, limit - sizes[sink]) // 2
    margin = jnp.where((source_of == ranking[0]) | (sink == ranking[0]) | (sizes[sink] == 0), 0, jnp.maximum(margin, 0))
    passed = jax.random.randint(jax.random.fold_in(own, 4), (count // 2,), 0, 1 << 20) % (margin + 1)
    sizes = sizes.at[source_of].add(-passed).at[sink].add(passed)
    items = jnp.searchsorted(jnp.cumsum(sizes), jnp.arange(rows * top), side="right").astype(jnp.int32)
    table = items.reshape(top, rows).T
    table = table[jax.random.permutation(jax.random.fold_in(own, 1), rows)]
    offset_by = jax.random.randint(jax.random.fold_in(own, 2), (rows, 1), 0, top)
    return jnp.take_along_axis(table, (jnp.arange(top)[None, :] + offset_by) % top, axis=1)


def portions_of(count, total, reach, lean, full):
    weights = [(1 << 20) // math.isqrt(grade ** lean) + 1 for grade in range(1, count + 1)]
    largest = reach if full else min(reach, max(-(-total // count), total * weights[0] // sum(weights)))
    least = 1 if total - largest >= count - 1 else 0
    counts, surplus = [largest] + [least] * (count - 1), total - largest - least * (count - 1)
    while surplus > 0:
        movable = [i for i in range(1, count) if counts[i] < largest] or [i for i in range(1, count) if counts[i] < reach]
        whole, remaining = sum([weights[i] for i in movable]), surplus
        for i in movable:
            extra = min(reach - counts[i], max(1, remaining * weights[i] // whole), surplus)
            counts[i] = counts[i] + extra
            surplus = surplus - extra
    return np.array(counts)


def gaussian(own_key, shape, deviation, bound, cuts=(), held_as=jnp.bfloat16):
    entries = deviation * jax.random.normal(own_key, shape, jnp.float32)
    if cuts:
        entries = entries * block_scale(own_key, shape, cuts, -0.22, 0.18)
    return jnp.clip(entries, -bound, bound).astype(held_as)


def setup_inputs(seed: int = 0) -> dict:
    key_list = jax.random.split(jax.random.key(seed), 14)
    layer_input = draw_layer_input(jax.random.fold_in(key_list[13], 71), 0)
    attn_gain = jnp.clip(1.0 + 0.18 * jax.random.normal(key_list[1], (D,), jnp.float32), 0.1, 1.9)
    query_weight = gaussian(key_list[2], (D, QH * HD), D ** -0.5, 0.109375, ((1, 16),))
    keyval_weight = gaussian(key_list[3], (D, 2 * KVH * HD), (D // 6) ** -0.5, 0.25)
    output_weight = gaussian(key_list[4], (QH * HD, D), (QH * HD // 2) ** -0.5, 0.125, ((0, 16),))
    cache_entries = draw_cache_entries(jax.random.fold_in(key_list[13], 71), 0)
    cache_length = draw_cache_length(jax.random.fold_in(key_list[13], 71), 0)
    expert_gain = jnp.clip(1.0 + 0.18 * jax.random.normal(key_list[7], (D,), jnp.float32), 0.1, 1.9)
    router_weight = draw_router_weight(jax.random.fold_in(key_list[13], 71), 0)
    expert_choice_keys = jax.random.split(jax.random.fold_in(key_list[9], 1), TOKENS // (ROWS // N_TP))
    expert_choice_turns = jax.random.permutation(jax.random.fold_in(key_list[9], 3), TOKENS // (ROWS // N_TP))
    expert_choice = jax.vmap(lambda own, number: shared_out(jax.random.fold_in(key_list[9], 2), own, number, ROWS // N_TP, E, TOPK, CAP, 1))(expert_choice_keys, expert_choice_turns).reshape((TOKENS, TOPK))
    gate_weight = gaussian(key_list[10], (E * FSPLIT, D, HBLOCK), D ** -0.5, 0.109375, ((0, 128),))
    up_weight = gaussian(key_list[11], (E * FSPLIT, D, HBLOCK), D ** -0.5, 0.109375, ((0, 128),))
    down_weight = gaussian(key_list[12], (E * FSPLIT, HBLOCK, D), FF ** -0.5, 0.109375, ((0, 128),))
    return {"layer_input": layer_input, "attn_gain": attn_gain, "query_weight": query_weight, "keyval_weight": keyval_weight, "output_weight": output_weight, "cache_entries": cache_entries, "cache_length": cache_length, "expert_gain": expert_gain, "router_weight": router_weight, "expert_choice": expert_choice, "gate_weight": gate_weight, "up_weight": up_weight, "down_weight": down_weight}


epsilon = 1e-05
rope_base = 150000.0

def rms_scale(row_block, gain_vector):
    values = row_block.astype(jnp.float32)
    inverse = lax.rsqrt(lax.optimization_barrier(jnp.mean(values * values, axis=-1, keepdims=True)) + epsilon)
    return (values * inverse * gain_vector.astype(jnp.float32)).astype(jnp.bfloat16)

def rotate(values, positions):
    half_dim = values.shape[-1] // 2
    frequency = rope_base ** (-jnp.arange(half_dim, dtype=jnp.float32) * 2.0 / values.shape[-1])
    angles = positions[:, None] * frequency[None, :]
    cosine = jnp.cos(angles)[:, None, :]
    sine_part = jnp.sin(angles)[:, None, :]
    front_part = values[..., :half_dim]
    back_part = values[..., half_dim:]
    return jnp.concatenate([front_part * cosine - back_part * sine_part, back_part * cosine + front_part * sine_part], axis=-1)

def reference(layer_input, attn_gain, query_weight, keyval_weight, output_weight, cache_entries, cache_length, expert_gain, router_weight, expert_choice, gate_weight, up_weight, down_weight):
    normed_in = rms_scale(layer_input, attn_gain)
    offsets = jnp.repeat(cache_length.astype(jnp.int32), ROWS)
    positions = (offsets + jnp.tile(jnp.arange(ROWS, dtype=jnp.int32), N_GRP)).astype(jnp.float32)
    query_out = jnp.dot(normed_in, query_weight, preferred_element_type=jnp.float32)
    queries = rotate(query_out.reshape(TOKENS, QH, HD), positions).astype(jnp.bfloat16)
    pair_out = jnp.dot(normed_in, keyval_weight, preferred_element_type=jnp.float32)
    new_keys = rotate(pair_out[:, :KVH * HD].reshape(TOKENS, KVH, HD), positions).astype(jnp.bfloat16)
    new_values = pair_out[:, KVH * HD:].reshape(TOKENS, KVH, HD).astype(jnp.bfloat16)
    caches = cache_entries.reshape(N_GRP, KVH, CTX, 2 * HD)
    per_group = QH // KVH
    queries_grouped = queries.reshape(N_GRP, ROWS, KVH, per_group, HD)
    keys_grouped = new_keys.reshape(N_GRP, ROWS, KVH, HD)
    values_grouped = new_values.reshape(N_GRP, ROWS, KVH, HD)
    causal = jnp.arange(ROWS)[:, None] >= jnp.arange(ROWS)[None, :]

    def one_head(item_index):
        group_index = item_index // KVH
        shared = item_index % KVH
        query_set = queries_grouped[group_index, :, shared].astype(jnp.float32)
        cached = caches[group_index, shared]
        keys_all = jnp.concatenate([cached[:, :HD], keys_grouped[group_index, :, shared]], axis=0).astype(jnp.float32)
        values_all = jnp.concatenate([cached[:, HD:], values_grouped[group_index, :, shared]], axis=0).astype(jnp.float32)
        cache_ok = jnp.arange(CTX, dtype=jnp.int32) < cache_length[group_index]
        allowed = jnp.concatenate([jnp.broadcast_to(cache_ok[None, :], (ROWS, CTX)), causal], axis=1)
        scores = jnp.einsum('nhd,kd->nhk', query_set, keys_all) * HD ** (-0.5)
        scores = jnp.where(allowed[:, None, :], scores, -jnp.inf)
        row_max = lax.optimization_barrier(jnp.max(scores, axis=-1, keepdims=True))
        weights = jnp.exp(scores - row_max)
        rounded = lax.optimization_barrier(weights.astype(jnp.bfloat16)).astype(jnp.float32)
        result = jnp.einsum('nhk,kd->nhd', rounded, values_all) / lax.optimization_barrier(jnp.sum(weights, axis=-1))[..., None]
        return result.astype(jnp.bfloat16)
    heads_out = lax.map(one_head, jnp.arange(N_GRP * KVH, dtype=jnp.int32))
    attended = heads_out.reshape(N_GRP, KVH, ROWS, per_group, HD).transpose(0, 2, 1, 3, 4).reshape(TOKENS, QH * HD)
    proj_out = jnp.dot(attended, output_weight, preferred_element_type=jnp.float32)
    hidden_state = (layer_input.astype(jnp.float32) + proj_out).astype(jnp.bfloat16)
    normed = rms_scale(hidden_state, expert_gain)
    logits = jnp.dot(normed, router_weight, preferred_element_type=jnp.float32)
    chosen = jnp.take_along_axis(logits, expert_choice, axis=1)
    route_weight = jax.nn.softmax(chosen, axis=-1).astype(jnp.bfloat16)
    block_rows = ROWS // N_TP
    block_total = TOKENS // block_rows
    expert_blocks = expert_choice.reshape(block_total, block_rows * TOPK)
    hit_table = (expert_blocks[:, :, None] == jnp.arange(E, dtype=jnp.int32)[None, None, :]).astype(jnp.int32)
    earlier = jnp.cumsum(hit_table, axis=1) - hit_table
    slot_index = lax.optimization_barrier(jnp.sum(earlier * hit_table, axis=2))
    target = expert_blocks * CAP + slot_index
    placed = target.reshape(block_total, block_rows, TOPK)[..., None] == jnp.arange(E * CAP, dtype=jnp.int32)
    dispatch = lax.optimization_barrier(jnp.sum(placed.astype(jnp.float32), axis=2))
    normed_blocks = normed.reshape(block_total, block_rows, D).astype(jnp.float32)
    buffers = jnp.einsum('brs,brd->bsd', dispatch, normed_blocks).astype(jnp.bfloat16)
    by_expert = buffers.reshape(block_total, E, CAP, D).transpose(1, 0, 2, 3).reshape(E, block_total * CAP, D)
    gate_blocks = gate_weight.reshape(E, FSPLIT, D, HBLOCK)
    up_blocks = up_weight.reshape(E, FSPLIT, D, HBLOCK)
    down_blocks = down_weight.reshape(E, FSPLIT, HBLOCK, D)

    def one_expert(item_index):
        rows_in = by_expert[item_index]
        gate_full = gate_blocks[item_index].transpose(1, 0, 2).reshape(D, FF)
        up_full = up_blocks[item_index].transpose(1, 0, 2).reshape(D, FF)
        gate_out = jnp.dot(rows_in, gate_full, preferred_element_type=jnp.float32)
        upper = jnp.dot(rows_in, up_full, preferred_element_type=jnp.float32)
        activated = (gate_out * jax.nn.sigmoid(1.702 * gate_out) * (upper + 1.0)).astype(jnp.bfloat16)
        pieces = jnp.einsum('sbf,bfd->sbd', activated.reshape(-1, FSPLIT, HBLOCK).astype(jnp.float32), down_blocks[item_index].astype(jnp.float32))
        rounded = lax.optimization_barrier(pieces.astype(jnp.bfloat16)).astype(jnp.float32)
        return lax.optimization_barrier(jnp.sum(rounded, axis=1)).astype(jnp.bfloat16)
    expert_out = lax.map(one_expert, jnp.arange(E, dtype=jnp.int32))
    gathered_back = expert_out.reshape(E, block_total, CAP, D).transpose(1, 0, 2, 3).reshape(block_total, E * CAP, D)
    combine = lax.optimization_barrier(jnp.sum(jnp.where(placed, route_weight.reshape(block_total, block_rows, TOPK)[..., None].astype(jnp.float32), 0.0), axis=2))
    mixture = jnp.einsum('brs,bsd->brd', combine, gathered_back.astype(jnp.float32))
    return (hidden_state.astype(jnp.float32) + mixture.reshape(TOKENS, D)).astype(jnp.bfloat16)
```

```python
import functools
import jax
import jax.numpy as jnp
from jax import lax
from jax.experimental import pallas as pl
from jax.experimental.pallas import tpu as pltpu

from jax.sharding import PartitionSpec as P

QH = 64
KVH = 8
HD = 64


epsilon = 1e-05
rope_base = 150000.0
mask_floor = -1e30


def from_partner(block, axis, apart):
    count = lax.axis_size(axis)
    route = []
    for low in range(count):
        high = low | 1 << apart
        if high != low and high < count:
            route += [(low, high), (high, low)]
    return lax.ppermute(block, axis, route)


def rms_scale(row_block, gain_vector):
    values = row_block.astype(jnp.float32)
    inverse = lax.rsqrt(jnp.mean(values * values, axis=-1, keepdims=True) + epsilon)
    return (values * inverse * gain_vector).astype(jnp.bfloat16)


def rotate(values, positions):
    half_dim = values.shape[-1] // 2
    frequency = rope_base ** (-jnp.arange(half_dim, dtype=jnp.float32) * 2.0 / values.shape[-1])
    angles = positions[:, None] * frequency[None, :]
    cosine = jnp.cos(angles)[:, None, :]
    sine_part = jnp.sin(angles)[:, None, :]
    front_part = values[..., :half_dim]
    back_part = values[..., half_dim:]
    return jnp.concatenate(
        [front_part * cosine - back_part * sine_part, back_part * cosine + front_part * sine_part],
        axis=-1,
    )


def attend_block(running, queries, keys_part, values_part, allowed):
    top_score, mass_sum, weighted = running
    scaling = queries.shape[-1] ** (-0.5)
    scores = (
        jnp.einsum("nhd,kd->nhk", queries, keys_part, preferred_element_type=jnp.float32) * scaling
    )
    scores = jnp.where(allowed, scores, mask_floor)
    new_max = jnp.maximum(top_score, jnp.max(scores, axis=-1))
    rescale = jnp.exp(top_score - new_max)
    weights = jnp.exp(scores - new_max[..., None])
    mass_sum = mass_sum * rescale + jnp.sum(weights, axis=-1)
    weighted = weighted * rescale[..., None] + jnp.einsum(
        "nhk,kd->nhd", weights.astype(jnp.bfloat16), values_part, preferred_element_type=jnp.float32
    )
    return (new_max, mass_sum, weighted)


def sweep(running, queries, entries, anchor, length):
    block_len = min(1024, entries.shape[0])
    head_dim = entries.shape[1] // 2
    block_count = jnp.clip(
        (length - anchor + block_len - 1) // block_len, 0, entries.shape[0] // block_len
    )

    def advance(block_index, carried):
        offset = block_index * block_len
        block_rows = lax.dynamic_slice_in_dim(entries, offset, block_len, 0)
        places = anchor + offset + jnp.arange(block_len, dtype=jnp.int32)
        allowed = (places < length)[None, None, :]
        return attend_block(
            carried, queries, block_rows[:, :head_dim], block_rows[:, head_dim:], allowed
        )

    return lax.fori_loop(jnp.int32(0), block_count, advance, running)


def fetch_keys(running, queries, own_entries, part_index, length):
    half_len = own_entries.shape[0]
    running = sweep(running, queries, own_entries, part_index * half_len, length)
    other_entries = from_partner(own_entries, "tp", 0)
    running = sweep(running, queries, other_entries, (1 - part_index) * half_len, length)
    return running


MESH = pl.DeviceIdType.MESH


def place(Z):
    g, t = lax.axis_index("grp"), lax.axis_index("tp")
    return g // 2, g % 2, t // Z, t % Z


def seat(x, c, y, z, Z):
    return (x * 2 + c, y * Z + z)


def greet(devices):
    barrier = pltpu.get_barrier_semaphore()
    for device in devices:
        pl.semaphore_signal(barrier, inc=1, device_id=device, device_id_type=MESH)
    pl.semaphore_wait(barrier, len(devices))


def plane_partners(X, Y, Z):
    x, c, y, z = place(Z)
    found = [seat(x, 1 - c, y, z, Z)]
    found += [seat(x, c, y, (z + k) % Z, Z) for k in (1, 2, 3)]
    for i in range(X):
        for j in range(Y):
            if i or j:
                found.append(seat((x + i) % X, c, (y + j) % Y, z, Z))
    return found


def send(src, dst, send_sem, recv_sem, device):
    return pltpu.make_async_remote_copy(
        src_ref=src,
        dst_ref=dst,
        send_sem=send_sem,
        recv_sem=recv_sem,
        device_id=device,
        device_id_type=MESH,
    )


def dispatch_kernel(
    X, Y, Z, B,
    rows, pick_own, pick_far, router,
    arrived, logits,
    near, out_own, out_far,
    row_send, row_recv, own_send, own_recv, far_send, far_recv,
    up_send, up_recv, down_send, down_recv, local_sem,
):
    x, c, y, z = place(Z)
    XY = X * Y
    half = rows.shape[0]
    zf, zu, zd = (z + 2) % Z, (z + 1) % Z, (z + 3) % Z
    partner = seat(x, 1 - c, y, z, Z)
    far = seat(x, c, y, zf, Z)
    above = seat(x, c, y, zu, Z)
    below = seat(x, c, y, zd, Z)

    def block(zs, xs, ys):
        return pl.ds(pl.multiple_of((zs * XY + xs * Y + ys) * B, 8), B)

    def own_block(xs, ys):
        return pl.ds(pl.multiple_of((xs * Y + ys) * B, 8), B)

    greet(plane_partners(X, Y, Z))
    to_partner = send(rows, near.at[0], row_send.at[0], row_recv.at[0], partner)
    to_far = send(rows, near.at[1], row_send.at[1], row_recv.at[1], far)
    to_partner.start()
    to_far.start()

    def scatter(pick, first, second, out, zs, send_sems, recv_sems):
        def one(i, carry):
            xi = lax.rem(x + i, X)
            here = pl.ds(pl.multiple_of(xi * Y * B, 8), Y * B)
            out[here, :] = (
                jnp.dot(pick[here, :half], first[...], preferred_element_type=jnp.float32)
                + jnp.dot(pick[here, half:], second[...], preferred_element_type=jnp.float32)
            ).astype(jnp.bfloat16)
            for j in range(Y):
                yj = lax.rem(y + j, Y)

                def go():
                    send(
                        out.at[own_block(xi, yj), :],
                        arrived.at[block(zs, x, y), :],
                        send_sems.at[i * Y + j],
                        recv_sems.at[i * Y + j],
                        seat(xi, c, yj, z, Z),
                    ).start()

                if j == 0:
                    pl.when(i > 0)(go)
                else:
                    go()
            return carry

        lax.fori_loop(0, X, one, 0)

    to_partner.wait_recv()
    scatter(pick_own, rows, near.at[0], out_own, z, own_send, own_recv)
    keep_own = pltpu.make_async_copy(
        out_own.at[own_block(x, y), :], arrived.at[block(z, x, y), :], local_sem.at[0]
    )
    keep_own.start()
    mine = out_own.at[own_block(x, y), :]
    send(mine, arrived.at[block(z, x, y), :], up_send.at[0], up_recv.at[0], above).start()
    send(mine, arrived.at[block(z, x, y), :], down_send.at[0], down_recv.at[0], below).start()

    to_far.wait_recv()
    far_partner = send(near.at[1], near.at[2], row_send.at[2], row_recv.at[2], partner)
    far_partner.start()
    far_partner.wait_recv()
    scatter(pick_far, near.at[1], near.at[2], out_far, zf, far_send, far_recv)
    keep_far = pltpu.make_async_copy(
        out_far.at[own_block(x, y), :], arrived.at[block(zf, x, y), :], local_sem.at[1]
    )
    keep_far.start()

    def source(k):
        i, j = k // Y, k % Y
        return lax.rem(x + X - i, X), lax.rem(y + Y - j, Y)

    def relay(k, carry):
        xs, ys = source(k)
        there = arrived.at[block(z, xs, ys), :]
        send(there, there, own_send.at[k], own_recv.at[k], above).wait_recv()
        send(there, there, up_send.at[k], up_recv.at[k], above).start()
        send(there, there, down_send.at[k], down_recv.at[k], below).start()
        return carry

    lax.fori_loop(1, XY, relay, 0)

    for part, held in enumerate((rows, near.at[0], near.at[1], near.at[2])):
        logits[part * half : (part + 1) * half, :] = lax.dot_general(
            held[...], router[...], (((1,), (1,)), ((), ())), preferred_element_type=jnp.float32
        )

    def finish(k, carry):
        xs, ys = source(k)
        at_far = arrived.at[block(zf, xs, ys), :]
        send(at_far, at_far, far_send.at[k], far_recv.at[k], above).wait()
        at_own = arrived.at[block(z, xs, ys), :]
        send(at_own, at_own, own_send.at[k], own_recv.at[k], above).wait_send()
        return carry

    lax.fori_loop(1, XY, finish, 0)

    def finish_z(k, carry):
        xs, ys = source(k)
        low = arrived.at[block(zd, xs, ys), :]
        send(low, low, up_send.at[k], up_recv.at[k], above).wait()
        high = arrived.at[block(zu, xs, ys), :]
        send(high, high, down_send.at[k], down_recv.at[k], below).wait()
        return carry

    lax.fori_loop(0, XY, finish_z, 0)
    keep_own.wait()
    keep_far.wait()
    to_partner.wait_send()
    to_far.wait_send()
    far_partner.wait_send()


def dispatch_rows(X, Y, Z, B, rows, pick_own, pick_far, router):
    half, width = rows.shape
    XY = X * Y
    vmem = pl.BlockSpec(memory_space=pltpu.VMEM)
    dma = pltpu.SemaphoreType.DMA
    return pl.pallas_call(
        functools.partial(dispatch_kernel, X, Y, Z, B),
        out_shape=(
            jax.ShapeDtypeStruct((Z * XY * B, width), jnp.bfloat16),
            jax.ShapeDtypeStruct((4 * half, router.shape[0]), jnp.float32),
        ),
        in_specs=[vmem] * 4,
        out_specs=(pl.BlockSpec(memory_space=pl.ANY), vmem),
        scratch_shapes=[
            pltpu.VMEM((3, half, width), jnp.bfloat16),
            pltpu.VMEM((XY * B, width), jnp.bfloat16),
            pltpu.VMEM((XY * B, width), jnp.bfloat16),
            dma((3,)), dma((3,)),
            dma((XY,)), dma((XY,)), dma((XY,)), dma((XY,)),
            dma((XY,)), dma((XY,)), dma((XY,)), dma((XY,)),
            dma((2,)),
        ],
        compiler_params=pltpu.CompilerParams(
            collective_id=3, has_side_effects=True, vmem_limit_bytes=40 * 1024 * 1024
        ),
        name="dispatch_rows",
    )(rows, pick_own, pick_far, router)


def return_kernel(
    X, Y, Z, B,
    pieces, logits, choice, slots, hidden,
    out,
    own, zin, summed, ret_own, ret_far, swap_out, swap_in, far_out, far_in,
    own_send, own_recv, far_send, far_recv,
    up_send, up_recv, down_send, down_recv, swap_send, swap_recv, local_sem,
):
    x, c, y, z = place(Z)
    XY = X * Y
    G = Y * B
    half, width = hidden.shape
    zf, zu, zd = (z + 2) % Z, (z + 1) % Z, (z + 3) % Z
    partner = seat(x, 1 - c, y, z, Z)
    far = seat(x, c, y, zf, Z)
    above = seat(x, c, y, zu, Z)
    below = seat(x, c, y, zd, Z)

    def block(zs, xs, ys):
        return pl.ds(pl.multiple_of((zs * XY + xs * Y + ys) * B, 8), B)

    def group(zs, xs):
        return pl.ds(pl.multiple_of((zs * XY + xs * Y) * B, 8), G)

    def own_block(xs, ys):
        return pl.ds(pl.multiple_of((xs * Y + ys) * B, 8), B)

    def own_group(xs):
        return pl.ds(pl.multiple_of(xs * Y * B, 8), G)

    greet(plane_partners(X, Y, Z))

    def z_copies(i):
        xi = lax.rem(x + i, X)
        here = own_group(xi)
        return (
            send(pieces.at[group(zu, xi), :], zin.at[0, here, :], up_send.at[i], up_recv.at[i], above),
            send(pieces.at[group(zd, xi), :], zin.at[1, here, :], down_send.at[i], down_recv.at[i], below),
            pltpu.make_async_copy(pieces.at[group(z, xi), :], own.at[here, :], local_sem.at[i]),
        )

    def start_z(i, carry):
        for copy in z_copies(i):
            copy.start()
        return carry

    lax.fori_loop(0, X, start_z, 0)

    def far_copy(k):
        xi, yj = lax.rem(x + k // Y, X), lax.rem(y + k % Y, Y)
        return send(
            pieces.at[block(zf, xi, yj), :],
            ret_far.at[own_block(x, y), :],
            far_send.at[k],
            far_recv.at[k],
            seat(xi, c, yj, z, Z),
        )

    def start_far(k, carry):
        far_copy(k).start()
        return carry

    lax.fori_loop(1, XY, start_far, 0)
    keep_far = pltpu.make_async_copy(
        pieces.at[block(zf, x, y), :], ret_far.at[own_block(x, y), :], local_sem.at[X]
    )
    keep_far.start()

    count, top = choice.shape
    experts = logits.shape[1]
    names = lax.broadcasted_iota(jnp.int32, (count, experts), 1)
    chosen = [
        jnp.sum(jnp.where(choice[:, k : k + 1] == names, logits[...], 0.0), axis=1, keepdims=True)
        for k in range(top)
    ]
    peak = functools.reduce(jnp.maximum, chosen)
    raised = [jnp.exp(value - peak) for value in chosen]
    total = functools.reduce(jnp.add, raised)
    places = lax.broadcasted_iota(jnp.int32, (count, XY * B), 1)
    spread = jnp.zeros((count, XY * B), jnp.float32)
    for k in range(top):
        weight = (raised[k] / total).astype(jnp.bfloat16).astype(jnp.float32)
        spread += jnp.where(slots[:, k : k + 1] == places, weight, 0.0)
    spread = spread.astype(jnp.bfloat16)

    def own_copy(i, j):
        xi, yj = lax.rem(x + i, X), lax.rem(y + j, Y)
        return send(
            summed.at[own_block(xi, yj), :],
            ret_own.at[own_block(x, y), :],
            own_send.at[i * Y + j],
            own_recv.at[i * Y + j],
            seat(xi, c, yj, z, Z),
        )

    def add_z(i, carry):
        for copy in z_copies(i)[:2]:
            copy.wait_recv()
        z_copies(i)[2].wait()
        here = own_group(lax.rem(x + i, X))
        summed[here, :] = (
            own[here, :].astype(jnp.float32)
            + zin[0, here, :].astype(jnp.float32)
            + zin[1, here, :].astype(jnp.float32)
        ).astype(jnp.bfloat16)
        for j in range(Y):
            if j == 0:
                pl.when(i > 0)(lambda: own_copy(i, 0).start())
            else:
                own_copy(i, j).start()
        return carry

    lax.fori_loop(0, X, add_z, 0)
    keep_own = pltpu.make_async_copy(
        summed.at[own_block(x, y), :], ret_own.at[own_block(x, y), :], local_sem.at[X + 1]
    )
    keep_own.start()

    def landed(ref, k):
        xs, ys = lax.rem(x + X - k // Y, X), lax.rem(y + Y - k % Y, Y)
        return ref.at[own_block(xs, ys), :]

    def wait_far(k, carry):
        there = landed(ret_far, k)
        send(there, there, far_send.at[k], far_recv.at[k], above).wait_recv()
        return carry

    lax.fori_loop(1, XY, wait_far, 0)
    keep_far.wait()
    swap_out[0] = jnp.dot(
        spread[3 * half :, :], ret_far[...], preferred_element_type=jnp.float32
    ).astype(jnp.bfloat16)
    swap_far = send(swap_out.at[0], swap_in.at[0], swap_send.at[0], swap_recv.at[0], partner)
    swap_far.start()
    far_sum = jnp.dot(spread[2 * half : 3 * half, :], ret_far[...], preferred_element_type=jnp.float32)
    swap_far.wait_recv()
    far_out[...] = (far_sum + swap_in[0].astype(jnp.float32)).astype(jnp.bfloat16)
    to_far = send(far_out, far_in, swap_send.at[1], swap_recv.at[1], far)
    to_far.start()

    def wait_own(k, carry):
        there = landed(ret_own, k)
        send(there, there, own_send.at[k], own_recv.at[k], above).wait_recv()
        return carry

    lax.fori_loop(1, XY, wait_own, 0)
    keep_own.wait()
    swap_out[1] = jnp.dot(
        spread[half : 2 * half, :], ret_own[...], preferred_element_type=jnp.float32
    ).astype(jnp.bfloat16)
    swap_own = send(swap_out.at[1], swap_in.at[1], swap_send.at[2], swap_recv.at[2], partner)
    swap_own.start()
    mixed = jnp.dot(spread[:half, :], ret_own[...], preferred_element_type=jnp.float32)
    to_far.wait_recv()
    swap_own.wait_recv()
    out[...] = (
        hidden[...].astype(jnp.float32)
        + (mixed + swap_in[1].astype(jnp.float32) + far_in[...].astype(jnp.float32))
    ).astype(jnp.bfloat16)

    def finish(k, carry):
        far_copy(k).wait_send()
        own_copy(k // Y, k % Y).wait_send()
        return carry

    lax.fori_loop(1, XY, finish, 0)

    def finish_z(i, carry):
        for copy in z_copies(i)[:2]:
            copy.wait_send()
        return carry

    lax.fori_loop(0, X, finish_z, 0)
    swap_far.wait_send()
    to_far.wait_send()
    swap_own.wait_send()


def return_rows(X, Y, Z, B, pieces, logits, choice, slots, hidden):
    half, width = hidden.shape
    XY = X * Y
    vmem = pl.BlockSpec(memory_space=pltpu.VMEM)
    dma = pltpu.SemaphoreType.DMA
    slab = pltpu.VMEM((XY * B, width), jnp.bfloat16)
    return pl.pallas_call(
        functools.partial(return_kernel, X, Y, Z, B),
        out_shape=jax.ShapeDtypeStruct((half, width), jnp.bfloat16),
        in_specs=[pl.BlockSpec(memory_space=pl.ANY)] + [vmem] * 4,
        out_specs=vmem,
        scratch_shapes=[
            slab,
            pltpu.VMEM((2, XY * B, width), jnp.bfloat16),
            slab, slab, slab,
            pltpu.VMEM((2, half, width), jnp.bfloat16),
            pltpu.VMEM((2, half, width), jnp.bfloat16),
            pltpu.VMEM((half, width), jnp.bfloat16),
            pltpu.VMEM((half, width), jnp.bfloat16),
            dma((XY,)), dma((XY,)), dma((XY,)), dma((XY,)),
            dma((X,)), dma((X,)), dma((X,)), dma((X,)),
            dma((3,)), dma((3,)), dma((X + 2,)),
        ],
        compiler_params=pltpu.CompilerParams(
            collective_id=4, has_side_effects=True, vmem_limit_bytes=48 * 1024 * 1024
        ),
        name="return_rows",
    )(pieces, logits, choice, slots, hidden)


def grp_tp_perm(count, mask):
    return [(low, low ^ mask) for low in range(count)]


def moe(hidden_state, normed, router_weight, target, gate_weight, up_weight, down_weight, X, Y, Z, capacity):
    c = lax.axis_index("grp") % 2
    count = X * 2 * Y * Z
    core_bit = Y * Z
    axes = ("grp", "tp")
    plain = [target]
    for mask in (core_bit, 2, core_bit | 2):
        plain.append(lax.ppermute(target, axes, grp_tp_perm(count, mask)))
    block = 2 * capacity
    half = target.shape[0]
    choice, slots = [], []
    for part, held in enumerate(plain):
        expert = held // capacity
        slot = held - expert * capacity
        core = c if part % 2 == 0 else 1 - c
        at = (expert // (2 * Y) * Y + expert % Y) * block + core * capacity + slot
        slots.append(jnp.where(expert // Y % 2 == c, at, -1))
        choice.append(expert)
    choice = jnp.concatenate(choice, axis=0)
    slots = jnp.concatenate(slots, axis=0)
    spots = X * Y * block
    picks = jnp.any(
        slots[None, :, :] == jnp.arange(spots, dtype=jnp.int32)[:, None, None], axis=-1
    ).astype(jnp.bfloat16)
    arrived, logits = dispatch_rows(
        X, Y, Z, block, normed, picks[:, : 2 * half], picks[:, 2 * half :], router_weight.T
    )
    gate_out = jnp.dot(arrived, gate_weight, preferred_element_type=jnp.float32)
    upper = jnp.dot(arrived, up_weight, preferred_element_type=jnp.float32)
    activated = (gate_out * jax.nn.sigmoid(1.702 * gate_out) * (upper + 1.0)).astype(jnp.bfloat16)
    pieces = jnp.dot(activated, down_weight, preferred_element_type=jnp.float32).astype(jnp.bfloat16)
    return return_rows(X, Y, Z, block, pieces, logits, choice, slots, hidden_state)


def local(
    layer_input,
    attn_gain,
    query_weight,
    keyval_weight,
    output_weight,
    cache_entries,
    cache_length,
    expert_gain,
    router_weight,
    expert_choice,
    gate_weight,
    up_weight,
    down_weight,
):
    tp_count = lax.axis_size("tp")
    tp_rank = lax.axis_index("tp")
    grp_count = lax.axis_size("grp")
    heads_here = query_weight.shape[1] // HD
    per_group = QH // KVH
    shared_head = tp_rank * heads_here // per_group
    key_columns = lax.dynamic_slice_in_dim(keyval_weight, shared_head * HD, HD, 1)
    value_columns = lax.dynamic_slice_in_dim(keyval_weight, KVH * HD + shared_head * HD, HD, 1)
    joined = jnp.concatenate([query_weight, key_columns, value_columns], axis=1)
    projected = jnp.dot(
        rms_scale(lax.all_gather(layer_input, "tp", axis=0, tiled=True), attn_gain),
        joined,
        preferred_element_type=jnp.float32,
    )
    rows_total = projected.shape[0]
    query_width = heads_here * HD
    length = cache_length[0]
    positions = (length + jnp.arange(rows_total, dtype=jnp.int32)).astype(jnp.float32)
    queries = rotate(
        projected[:, :query_width].reshape(rows_total, heads_here, HD), positions
    ).astype(jnp.bfloat16)
    new_keys = rotate(projected[:, query_width : query_width + HD][:, None, :], positions)[
        :, 0, :
    ].astype(jnp.bfloat16)
    new_values = projected[:, query_width + HD :].astype(jnp.bfloat16)
    initial_state = (
        jnp.full((rows_total, heads_here), mask_floor, jnp.float32),
        jnp.zeros((rows_total, heads_here), jnp.float32),
        jnp.zeros((rows_total, heads_here, HD), jnp.float32),
    )
    causal = (jnp.arange(rows_total)[:, None] >= jnp.arange(rows_total)[None, :])[:, None, :]
    running = attend_block(initial_state, queries, new_keys, new_values, causal)
    splits = tp_count // KVH
    part_index = tp_rank % splits
    own_entries = cache_entries[0, 0]
    running = fetch_keys(running, queries, own_entries, part_index, length)
    attended = (
        (running[2] / running[1][..., None]).astype(jnp.bfloat16).reshape(rows_total, query_width)
    )
    local_rows = layer_input.shape[0]
    proj_out = lax.psum_scatter(
        jnp.dot(attended, output_weight, preferred_element_type=jnp.float32).astype(jnp.bfloat16),
        "tp",
        scatter_dimension=0,
        tiled=True,
    ).astype(jnp.float32)
    hidden_state = (layer_input.astype(jnp.float32) + proj_out).astype(jnp.bfloat16)
    normed = rms_scale(hidden_state, expert_gain)
    expert_total = router_weight.shape[1]
    top_count = expert_choice.shape[1]
    capacity = max(2, 3 * top_count * local_rows // (2 * expert_total))
    across = tp_count * grp_count // expert_total
    picked = expert_choice[:, :, None] == jnp.arange(expert_total, dtype=jnp.int32)[None, None, :]
    flat_hits = picked.reshape(local_rows * top_count, expert_total).astype(jnp.int32)
    earlier = jnp.cumsum(flat_hits, axis=0) - flat_hits
    slot_index = jnp.sum(earlier * flat_hits, axis=1).reshape(local_rows, top_count)
    target = expert_choice * capacity + slot_index
    return moe(
        hidden_state,
        normed,
        router_weight,
        target,
        gate_weight[0],
        up_weight[0],
        down_weight[0],
        grp_count // 2,
        tp_count // across,
        across,
        capacity,
    )


def solution(mesh):
    placed = (
        P(("grp", "tp"), None),
        P(),
        P(None, "tp"),
        P(),
        P("tp", None),
        P("grp", "tp", None, None),
        P("grp"),
        P(),
        P(),
        P(("grp", "tp"), None),
        P(("grp", "tp"), None, None),
        P(("grp", "tp"), None, None),
        P(("grp", "tp"), None, None),
    )
    return jax.shard_map(
        local, mesh=mesh, in_specs=placed, out_specs=P(("grp", "tp"), None), check_vma=False
    )
```

```python
import functools
import jax
import jax.numpy as jnp
from jax import lax
from jax.experimental import pallas as pl
from jax.experimental.pallas import tpu as pltpu

from jax.sharding import PartitionSpec as P

QH = 64
KVH = 8
HD = 64


epsilon = 1e-05
rope_base = 150000.0
mask_floor = -1e30


def from_partner(block, axis, apart):
    count = lax.axis_size(axis)
    route = []
    for low in range(count):
        high = low | 1 << apart
        if high != low and high < count:
            route += [(low, high), (high, low)]
    return lax.ppermute(block, axis, route)


def rms_scale(row_block, gain_vector):
    values = row_block.astype(jnp.float32)
    inverse = lax.rsqrt(jnp.mean(values * values, axis=-1, keepdims=True) + epsilon)
    return (values * inverse * gain_vector).astype(jnp.bfloat16)


def rotate(values, positions):
    half_dim = values.shape[-1] // 2
    frequency = rope_base ** (-jnp.arange(half_dim, dtype=jnp.float32) * 2.0 / values.shape[-1])
    angles = positions[:, None] * frequency[None, :]
    cosine = jnp.cos(angles)[:, None, :]
    sine_part = jnp.sin(angles)[:, None, :]
    front_part = values[..., :half_dim]
    back_part = values[..., half_dim:]
    return jnp.concatenate(
        [front_part * cosine - back_part * sine_part, back_part * cosine + front_part * sine_part],
        axis=-1,
    )


def attend_block(running, queries, keys_part, values_part, allowed):
    top_score, mass_sum, weighted = running
    scaling = queries.shape[-1] ** (-0.5)
    scores = (
        jnp.einsum("nhd,kd->nhk", queries, keys_part, preferred_element_type=jnp.float32) * scaling
    )
    scores = jnp.where(allowed, scores, mask_floor)
    new_max = jnp.maximum(top_score, jnp.max(scores, axis=-1))
    rescale = jnp.exp(top_score - new_max)
    weights = jnp.exp(scores - new_max[..., None])
    mass_sum = mass_sum * rescale + jnp.sum(weights, axis=-1)
    weighted = weighted * rescale[..., None] + jnp.einsum(
        "nhk,kd->nhd", weights.astype(jnp.bfloat16), values_part, preferred_element_type=jnp.float32
    )
    return (new_max, mass_sum, weighted)


def sweep(running, queries, entries, anchor, length):
    block_len = min(1024, entries.shape[0])
    head_dim = entries.shape[1] // 2
    block_count = jnp.clip(
        (length - anchor + block_len - 1) // block_len, 0, entries.shape[0] // block_len
    )

    def advance(block_index, carried):
        offset = block_index * block_len
        block_rows = lax.dynamic_slice_in_dim(entries, offset, block_len, 0)
        places = anchor + offset + jnp.arange(block_len, dtype=jnp.int32)
        allowed = (places < length)[None, None, :]
        return attend_block(
            carried, queries, block_rows[:, :head_dim], block_rows[:, head_dim:], allowed
        )

    return lax.fori_loop(jnp.int32(0), block_count, advance, running)


def fetch_keys(running, queries, own_entries, part_index, length):
    half_len = own_entries.shape[0]
    running = sweep(running, queries, own_entries, part_index * half_len, length)
    other_entries = from_partner(own_entries, "tp", 0)
    running = sweep(running, queries, other_entries, (1 - part_index) * half_len, length)
    return running


MESH = pl.DeviceIdType.MESH


def place(Z):
    g, t = lax.axis_index("grp"), lax.axis_index("tp")
    return g // 2, g % 2, t // Z, t % Z


def seat(x, c, y, z, Z):
    return (x * 2 + c, y * Z + z)


def greet(devices):
    barrier = pltpu.get_barrier_semaphore()
    for device in devices:
        pl.semaphore_signal(barrier, inc=1, device_id=device, device_id_type=MESH)
    pl.semaphore_wait(barrier, len(devices))


def plane_partners(X, Y, Z):
    x, c, y, z = place(Z)
    found = [seat(x, 1 - c, y, z, Z)]
    found += [seat(x, c, y, (z + k) % Z, Z) for k in (1, 2, 3)]
    for i in range(X):
        for j in range(Y):
            if i or j:
                found.append(seat((x + i) % X, c, (y + j) % Y, z, Z))
    return found


def send(src, dst, send_sem, recv_sem, device):
    return pltpu.make_async_remote_copy(
        src_ref=src,
        dst_ref=dst,
        send_sem=send_sem,
        recv_sem=recv_sem,
        device_id=device,
        device_id_type=MESH,
    )


def dispatch_kernel(
    X, Y, Z, B,
    rows, pick_own, pick_far, router,
    arrived, logits,
    near, out_own, out_far,
    row_send, row_recv, own_send, own_recv, far_send, far_recv,
    up_send, up_recv, down_send, down_recv, local_sem,
):
    x, c, y, z = place(Z)
    XY = X * Y
    half = rows.shape[0]
    zf, zu, zd = (z + 2) % Z, (z + 1) % Z, (z + 3) % Z
    partner = seat(x, 1 - c, y, z, Z)
    far = seat(x, c, y, zf, Z)
    above = seat(x, c, y, zu, Z)
    below = seat(x, c, y, zd, Z)

    def block(zs, xs, ys):
        return pl.ds(pl.multiple_of((zs * XY + xs * Y + ys) * B, 8), B)

    def own_block(xs, ys):
        return pl.ds(pl.multiple_of((xs * Y + ys) * B, 8), B)

    greet(plane_partners(X, Y, Z))
    to_partner = send(rows, near.at[0], row_send.at[0], row_recv.at[0], partner)
    to_far = send(rows, near.at[1], row_send.at[1], row_recv.at[1], far)
    to_partner.start()
    to_far.start()

    def scatter(pick, first, second, out, zs, send_sems, recv_sems):
        def one(i, carry):
            xi = lax.rem(x + i, X)
            here = pl.ds(pl.multiple_of(xi * Y * B, 8), Y * B)
            out[here, :] = (
                jnp.dot(pick[here, :half], first[...], preferred_element_type=jnp.float32)
                + jnp.dot(pick[here, half:], second[...], preferred_element_type=jnp.float32)
            ).astype(jnp.bfloat16)
            for j in range(Y):
                yj = lax.rem(y + j, Y)

                def go():
                    send(
                        out.at[own_block(xi, yj), :],
                        arrived.at[block(zs, x, y), :],
                        send_sems.at[i * Y + j],
                        recv_sems.at[i * Y + j],
                        seat(xi, c, yj, z, Z),
                    ).start()

                if j == 0:
                    pl.when(i > 0)(go)
                else:
                    go()
            return carry

        lax.fori_loop(0, X, one, 0)

    to_partner.wait_recv()
    scatter(pick_own, rows, near.at[0], out_own, z, own_send, own_recv)
    keep_own = pltpu.make_async_copy(
        out_own.at[own_block(x, y), :], arrived.at[block(z, x, y), :], local_sem.at[0]
    )
    keep_own.start()
    mine = out_own.at[own_block(x, y), :]
    send(mine, arrived.at[block(z, x, y), :], up_send.at[0], up_recv.at[0], above).start()
    send(mine, arrived.at[block(z, x, y), :], down_send.at[0], down_recv.at[0], below).start()

    to_far.wait_recv()
    far_partner = send(near.at[1], near.at[2], row_send.at[2], row_recv.at[2], partner)
    far_partner.start()
    far_partner.wait_recv()
    scatter(pick_far, near.at[1], near.at[2], out_far, zf, far_send, far_recv)
    keep_far = pltpu.make_async_copy(
        out_far.at[own_block(x, y), :], arrived.at[block(zf, x, y), :], local_sem.at[1]
    )
    keep_far.start()

    def source(k):
        i, j = k // Y, k % Y
        return lax.rem(x + X - i, X), lax.rem(y + Y - j, Y)

    def relay(k, carry):
        xs, ys = source(k)
        there = arrived.at[block(z, xs, ys), :]
        send(there, there, own_send.at[k], own_recv.at[k], above).wait_recv()
        send(there, there, up_send.at[k], up_recv.at[k], above).start()
        send(there, there, down_send.at[k], down_recv.at[k], below).start()
        return carry

    lax.fori_loop(1, XY, relay, 0)

    for part, held in enumerate((rows, near.at[0], near.at[1], near.at[2])):
        logits[part * half : (part + 1) * half, :] = lax.dot_general(
            held[...], router[...], (((1,), (1,)), ((), ())), preferred_element_type=jnp.float32
        )

    def finish(k, carry):
        xs, ys = source(k)
        at_far = arrived.at[block(zf, xs, ys), :]
        send(at_far, at_far, far_send.at[k], far_recv.at[k], above).wait()
        at_own = arrived.at[block(z, xs, ys), :]
        send(at_own, at_own, own_send.at[k], own_recv.at[k], above).wait_send()
        return carry

    lax.fori_loop(1, XY, finish, 0)

    def finish_z(k, carry):
        xs, ys = source(k)
        low = arrived.at[block(zd, xs, ys), :]
        send(low, low, up_send.at[k], up_recv.at[k], above).wait()
        high = arrived.at[block(zu, xs, ys), :]
        send(high, high, down_send.at[k], down_recv.at[k], below).wait()
        return carry

    lax.fori_loop(0, XY, finish_z, 0)
    keep_own.wait()
    keep_far.wait()
    to_partner.wait_send()
    to_far.wait_send()
    far_partner.wait_send()


def dispatch_rows(X, Y, Z, B, rows, pick_own, pick_far, router):
    half, width = rows.shape
    XY = X * Y
    vmem = pl.BlockSpec(memory_space=pltpu.VMEM)
    dma = pltpu.SemaphoreType.DMA
    return pl.pallas_call(
        functools.partial(dispatch_kernel, X, Y, Z, B),
        out_shape=(
            jax.ShapeDtypeStruct((Z * XY * B, width), jnp.bfloat16),
            jax.ShapeDtypeStruct((4 * half, router.shape[0]), jnp.float32),
        ),
        in_specs=[vmem] * 4,
        out_specs=(pl.BlockSpec(memory_space=pl.ANY), vmem),
        scratch_shapes=[
            pltpu.VMEM((3, half, width), jnp.bfloat16),
            pltpu.VMEM((XY * B, width), jnp.bfloat16),
            pltpu.VMEM((XY * B, width), jnp.bfloat16),
            dma((3,)), dma((3,)),
            dma((XY,)), dma((XY,)), dma((XY,)), dma((XY,)),
            dma((XY,)), dma((XY,)), dma((XY,)), dma((XY,)),
            dma((2,)),
        ],
        compiler_params=pltpu.CompilerParams(
            collective_id=3, has_side_effects=True, vmem_limit_bytes=40 * 1024 * 1024
        ),
        name="dispatch_rows",
    )(rows, pick_own, pick_far, router)


def return_kernel(
    X, Y, Z, B,
    pieces, logits, choice, slots, hidden,
    out,
    own, zin, summed, ret_own, ret_far, swap_out, swap_in, far_out, far_in,
    own_send, own_recv, far_send, far_recv,
    up_send, up_recv, down_send, down_recv, swap_send, swap_recv, local_sem,
):
    x, c, y, z = place(Z)
    XY = X * Y
    G = Y * B
    half, width = hidden.shape
    zf, zu, zd = (z + 2) % Z, (z + 1) % Z, (z + 3) % Z
    partner = seat(x, 1 - c, y, z, Z)
    far = seat(x, c, y, zf, Z)
    above = seat(x, c, y, zu, Z)
    below = seat(x, c, y, zd, Z)

    def block(zs, xs, ys):
        return pl.ds(pl.multiple_of((zs * XY + xs * Y + ys) * B, 8), B)

    def group(zs, xs):
        return pl.ds(pl.multiple_of((zs * XY + xs * Y) * B, 8), G)

    def own_block(xs, ys):
        return pl.ds(pl.multiple_of((xs * Y + ys) * B, 8), B)

    def own_group(xs):
        return pl.ds(pl.multiple_of(xs * Y * B, 8), G)

    greet(plane_partners(X, Y, Z))

    def z_copies(i):
        xi = lax.rem(x + i, X)
        here = own_group(xi)
        return (
            send(pieces.at[group(zu, xi), :], zin.at[0, here, :], up_send.at[i], up_recv.at[i], above),
            send(pieces.at[group(zd, xi), :], zin.at[1, here, :], down_send.at[i], down_recv.at[i], below),
            pltpu.make_async_copy(pieces.at[group(z, xi), :], own.at[here, :], local_sem.at[i]),
        )

    def start_z(i, carry):
        for copy in z_copies(i):
            copy.start()
        return carry

    lax.fori_loop(0, X, start_z, 0)

    def far_copy(k):
        xi, yj = lax.rem(x + k // Y, X), lax.rem(y + k % Y, Y)
        return send(
            pieces.at[block(zf, xi, yj), :],
            ret_far.at[own_block(x, y), :],
            far_send.at[k],
            far_recv.at[k],
            seat(xi, c, yj, z, Z),
        )

    def start_far(k, carry):
        far_copy(k).start()
        return carry

    lax.fori_loop(1, XY, start_far, 0)
    keep_far = pltpu.make_async_copy(
        pieces.at[block(zf, x, y), :], ret_far.at[own_block(x, y), :], local_sem.at[X]
    )
    keep_far.start()

    count, top = choice.shape
    experts = logits.shape[1]
    names = lax.broadcasted_iota(jnp.int32, (count, experts), 1)
    chosen = [
        jnp.sum(jnp.where(choice[:, k : k + 1] == names, logits[...], 0.0), axis=1, keepdims=True)
        for k in range(top)
    ]
    peak = functools.reduce(jnp.maximum, chosen)
    raised = [jnp.exp(value - peak) for value in chosen]
    total = functools.reduce(jnp.add, raised)
    places = lax.broadcasted_iota(jnp.int32, (count, XY * B), 1)
    spread = jnp.zeros((count, XY * B), jnp.float32)
    for k in range(top):
        weight = (raised[k] / total).astype(jnp.bfloat16).astype(jnp.float32)
        spread += jnp.where(slots[:, k : k + 1] == places, weight, 0.0)
    spread = spread.astype(jnp.bfloat16)

    def own_copy(i, j):
        xi, yj = lax.rem(x + i, X), lax.rem(y + j, Y)
        return send(
            summed.at[own_block(xi, yj), :],
            ret_own.at[own_block(x, y), :],
            own_send.at[i * Y + j],
            own_recv.at[i * Y + j],
            seat(xi, c, yj, z, Z),
        )

    def add_z(i, carry):
        for copy in z_copies(i)[:2]:
            copy.wait_recv()
        z_copies(i)[2].wait()
        here = own_group(lax.rem(x + i, X))
        summed[here, :] = (
            own[here, :].astype(jnp.float32)
            + zin[0, here, :].astype(jnp.float32)
            + zin[1, here, :].astype(jnp.float32)
        ).astype(jnp.bfloat16)
        for j in range(Y):
            if j == 0:
                pl.when(i > 0)(lambda: own_copy(i, 0).start())
            else:
                own_copy(i, j).start()
        return carry

    lax.fori_loop(0, X, add_z, 0)
    keep_own = pltpu.make_async_copy(
        summed.at[own_block(x, y), :], ret_own.at[own_block(x, y), :], local_sem.at[X + 1]
    )
    keep_own.start()

    def landed(ref, k):
        xs, ys = lax.rem(x + X - k // Y, X), lax.rem(y + Y - k % Y, Y)
        return ref.at[own_block(xs, ys), :]

    def wait_far(k, carry):
        there = landed(ret_far, k)
        send(there, there, far_send.at[k], far_recv.at[k], above).wait_recv()
        return carry

    lax.fori_loop(1, XY, wait_far, 0)
    keep_far.wait()
    swap_out[0] = jnp.dot(
        spread[3 * half :, :], ret_far[...], preferred_element_type=jnp.float32
    ).astype(jnp.bfloat16)
    swap_far = send(swap_out.at[0], swap_in.at[0], swap_send.at[0], swap_recv.at[0], partner)
    swap_far.start()
    far_sum = jnp.dot(spread[2 * half : 3 * half, :], ret_far[...], preferred_element_type=jnp.float32)
    swap_far.wait_recv()
    far_out[...] = (far_sum + swap_in[0].astype(jnp.float32)).astype(jnp.bfloat16)
    to_far = send(far_out, far_in, swap_send.at[1], swap_recv.at[1], far)
    to_far.start()

    def wait_own(k, carry):
        there = landed(ret_own, k)
        send(there, there, own_send.at[k], own_recv.at[k], above).wait_recv()
        return carry

    lax.fori_loop(1, XY, wait_own, 0)
    keep_own.wait()
    swap_out[1] = jnp.dot(
        spread[half : 2 * half, :], ret_own[...], preferred_element_type=jnp.float32
    ).astype(jnp.bfloat16)
    swap_own = send(swap_out.at[1], swap_in.at[1], swap_send.at[2], swap_recv.at[2], partner)
    swap_own.start()
    mixed = jnp.dot(spread[:half, :], ret_own[...], preferred_element_type=jnp.float32)
    to_far.wait_recv()
    swap_own.wait_recv()
    out[...] = (
        hidden[...].astype(jnp.float32)
        + (mixed + swap_in[1].astype(jnp.float32) + far_in[...].astype(jnp.float32))
    ).astype(jnp.bfloat16)

    def finish(k, carry):
        far_copy(k).wait_send()
        own_copy(k // Y, k % Y).wait_send()
        return carry

    lax.fori_loop(1, XY, finish, 0)

    def finish_z(i, carry):
        for copy in z_copies(i)[:2]:
            copy.wait_send()
        return carry

    lax.fori_loop(0, X, finish_z, 0)
    swap_far.wait_send()
    to_far.wait_send()
    swap_own.wait_send()


def return_rows(X, Y, Z, B, pieces, logits, choice, slots, hidden):
    half, width = hidden.shape
    XY = X * Y
    vmem = pl.BlockSpec(memory_space=pltpu.VMEM)
    dma = pltpu.SemaphoreType.DMA
    slab = pltpu.VMEM((XY * B, width), jnp.bfloat16)
    return pl.pallas_call(
        functools.partial(return_kernel, X, Y, Z, B),
        out_shape=jax.ShapeDtypeStruct((half, width), jnp.bfloat16),
        in_specs=[pl.BlockSpec(memory_space=pl.ANY)] + [vmem] * 4,
        out_specs=vmem,
        scratch_shapes=[
            slab,
            pltpu.VMEM((2, XY * B, width), jnp.bfloat16),
            slab, slab, slab,
            pltpu.VMEM((2, half, width), jnp.bfloat16),
            pltpu.VMEM((2, half, width), jnp.bfloat16),
            pltpu.VMEM((half, width), jnp.bfloat16),
            pltpu.VMEM((half, width), jnp.bfloat16),
            dma((XY,)), dma((XY,)), dma((XY,)), dma((XY,)),
            dma((X,)), dma((X,)), dma((X,)), dma((X,)),
            dma((3,)), dma((3,)), dma((X + 2,)),
        ],
        compiler_params=pltpu.CompilerParams(
            collective_id=4, has_side_effects=True, vmem_limit_bytes=48 * 1024 * 1024
        ),
        name="return_rows",
    )(pieces, logits, choice, slots, hidden)


def grp_tp_perm(count, mask):
    return [(low, low ^ mask) for low in range(count)]


def moe(hidden_state, normed, router_weight, target, gate_weight, up_weight, down_weight, X, Y, Z, capacity):
    c = lax.axis_index("grp") % 2
    count = X * 2 * Y * Z
    core_bit = Y * Z
    axes = ("grp", "tp")
    plain = [target]
    for mask in (core_bit, 2, core_bit | 2):
        plain.append(lax.ppermute(target, axes, grp_tp_perm(count, mask)))
    block = 2 * capacity
    half = target.shape[0]
    choice, slots = [], []
    for part, held in enumerate(plain):
        expert = held // capacity
        slot = held - expert * capacity
        core = c if part % 2 == 0 else 1 - c
        at = (expert // (2 * Y) * Y + expert % Y) * block + core * capacity + slot
        slots.append(jnp.where(expert // Y % 2 == c, at, -1))
        choice.append(expert)
    choice = jnp.concatenate(choice, axis=0)
    slots = jnp.concatenate(slots, axis=0)
    spots = X * Y * block
    picks = jnp.any(
        slots[None, :, :] == jnp.arange(spots, dtype=jnp.int32)[:, None, None], axis=-1
    ).astype(jnp.bfloat16)
    arrived, logits = dispatch_rows(
        X, Y, Z, block, normed, picks[:, : 2 * half], picks[:, 2 * half :], router_weight.T
    )
    gate_out = jnp.dot(arrived, gate_weight, preferred_element_type=jnp.float32)
    upper = jnp.dot(arrived, up_weight, preferred_element_type=jnp.float32)
    activated = (gate_out * jax.nn.sigmoid(1.702 * gate_out) * (upper + 1.0)).astype(jnp.bfloat16)
    pieces = jnp.dot(activated, down_weight, preferred_element_type=jnp.float32).astype(jnp.bfloat16)
    return return_rows(X, Y, Z, block, pieces, logits, choice, slots, hidden_state)


def gather_kernel(
    Y, Z,
    rows,
    whole,
    first_send, first_recv, relay_send, relay_recv,
    second_send, second_recv, pass_send, pass_recv, local_sem,
):
    x, c, y, z = place(Z)
    half = rows.shape[0] // 2
    quarter = half // 2
    around = [[seat(x, c, y, (z + 1) % Z, Z), seat(x, c, y, (z + 3) % Z, Z)],
              [seat(x, c, (y + 1) % Y, z, Z), seat(x, c, (y + 3) % Y, z, Z)]]
    greet(around[0] + around[1])

    def block(way, far, near):
        if way == 0:
            return ((y + far) % Y) * Z + (z + near) % Z
        return ((y + near) % Y) * Z + (z + far) % Z

    def part(way, far, near, start, size):
        return whole.at[block(way, far, near), pl.ds(way * half + start, size), :]

    def first(way, side):
        there = part(way, 0, 0, 0, half)
        return send(
            rows.at[pl.ds(way * half, half), :], there,
            first_send.at[way, side], first_recv.at[way, side], around[way][side],
        )

    def first_landed(way, side):
        there = part(way, 0, (3, 1)[side], 0, half)
        return send(there, there, first_send.at[way, side], first_recv.at[way, side], around[way][side])

    def relay(way, side):
        there = part(way, 0, (3, 1)[side], side * quarter, quarter)
        return send(there, there, relay_send.at[way, side], relay_recv.at[way, side], around[way][side])

    def relay_landed(way, side):
        there = part(way, 0, 2, side * quarter, quarter)
        return send(there, there, relay_send.at[way, side], relay_recv.at[way, side], around[way][side])

    def second(way, side, near):
        there = part(way, 0, near, 0, half)
        src = rows.at[pl.ds(way * half, half), :] if near == 0 else there
        return send(
            src, there, second_send.at[way, side, near], second_recv.at[way, side, near],
            around[1 - way][side],
        )

    def second_landed(way, side, near):
        there = part(way, (3, 1)[side], near, 0, half)
        return send(
            there, there, second_send.at[way, side, near], second_recv.at[way, side, near],
            around[1 - way][side],
        )

    def onward(way, near):
        side = 0 if near in (0, 1) else 1
        there = part(way, (3, 1)[side], near, 0, half)
        return send(there, there, pass_send.at[way, near], pass_recv.at[way, near], around[1 - way][side])

    def onward_landed(way, near):
        there = part(way, 2, near, 0, half)
        return send(there, there, pass_send.at[way, near], pass_recv.at[way, near], around[1 - way][0])

    for way in (0, 1):
        for side in (0, 1):
            first(way, side).start()
    for way in (0, 1):
        for side in (0, 1):
            second(way, side, 0).start()
    keep = pltpu.make_async_copy(rows, whole.at[y * Z + z], local_sem.at[0])
    keep.start()
    for way in (0, 1):
        for side in (0, 1):
            first_landed(way, side).wait_recv()
            relay(way, side).start()
    for way in (0, 1):
        for near in (3, 1):
            for side in (0, 1):
                second(way, side, near).start()
    for near in (0,):
        for way in (0, 1):
            side = 0
            second_landed(way, side, near).wait_recv()
            onward(way, near).start()
    for way in (0, 1):
        for side in (0, 1):
            relay_landed(way, side).wait_recv()
        for side in (0, 1):
            second(way, side, 2).start()
    for near in (3, 1, 2):
        for way in (0, 1):
            side = 0 if near in (0, 1) else 1
            second_landed(way, side, near).wait_recv()
            onward(way, near).start()
    for way in (0, 1):
        for near in (0, 3, 1, 2):
            side = 1 if near in (0, 1) else 0
            second_landed(way, side, near).wait_recv()
            onward_landed(way, near).wait_recv()
    for way in (0, 1):
        for side in (0, 1):
            first(way, side).wait_send()
            relay(way, side).wait_send()
            for near in range(4):
                second(way, side, near).wait_send()
        for near in range(4):
            onward(way, near).wait_send()
    keep.wait()


def gather_rows(Y, Z, rows):
    dma = pltpu.SemaphoreType.DMA
    return pl.pallas_call(
        functools.partial(gather_kernel, Y, Z),
        out_shape=jax.ShapeDtypeStruct((Y * Z,) + rows.shape, rows.dtype),
        in_specs=[pl.BlockSpec(memory_space=pltpu.VMEM)],
        out_specs=pl.BlockSpec(memory_space=pl.ANY),
        scratch_shapes=[
            dma((2, 2)), dma((2, 2)), dma((2, 2)), dma((2, 2)),
            dma((2, 2, 4)), dma((2, 2, 4)), dma((2, 4)), dma((2, 4)), dma((1,)),
        ],
        compiler_params=pltpu.CompilerParams(collective_id=1, has_side_effects=True),
        name="gather_rows",
    )(rows)


def reduce_kernel(
    Y, Z,
    attended, weight, residual, gain,
    hidden, normed,
    terms, pass_in, join_in, halves, hop_in, end_in,
    pass_send, pass_recv, join_send, join_recv, hop_send, hop_recv, end_send, end_recv,
):
    x, c, y, z = place(Z)
    R = residual.shape[0]
    half = R // 2
    quarter = half // 2
    around = [[seat(x, c, (y + 1) % Y, z, Z), seat(x, c, (y + 3) % Y, z, Z)],
              [seat(x, c, y, (z + 1) % Z, Z), seat(x, c, y, (z + 3) % Z, Z)]]
    greet(around[0] + around[1])

    def block(way, ring, other):
        if way == 0:
            return ((y + ring) % Y) * Z + (z + other) % Z
        return ((y + other) % Y) * Z + (z + ring) % Z

    def term(way, ring, other):
        return terms.at[block(way, ring, other), pl.ds(way * half, half), :]

    def passing(way, other):
        side = 0 if other in (0, 1) else 1
        return send(
            term(way, 2, other), pass_in.at[way, other],
            pass_send.at[way, other], pass_recv.at[way, other], around[way][side],
        )

    def joining(way, side, other):
        return send(
            term(way, (1, 3)[side], other), join_in.at[way, side, other],
            join_send.at[way, side, other], join_recv.at[way, side, other], around[way][side],
        )

    def hop(way, side):
        return send(
            halves.at[way, 2, pl.ds(side * quarter, quarter), :], hop_in.at[way, side],
            hop_send.at[way, side], hop_recv.at[way, side], around[1 - way][side],
        )

    def ending(way, side):
        return send(
            halves.at[way, (1, 3)[side]], end_in.at[way, side],
            end_send.at[way, side], end_recv.at[way, side], around[1 - way][side],
        )

    def project(step):
        at = (y + step) % Y
        rows = pl.ds(pl.multiple_of(at * (Z * R), Z * R), Z * R)
        got = lax.dot_general(
            attended[rows, :], weight[...], (((1,), (1,)), ((), ())),
            preferred_element_type=jnp.float32,
        ).astype(jnp.bfloat16)
        terms[pl.ds(at * Z, Z)] = got.reshape(Z, R, got.shape[-1])

    project(2)
    for other in (2, 1, 3, 0):
        passing(0, other).start()
    project(1)
    project(3)
    project(0)
    for other in (2, 1, 3, 0):
        passing(1, other).start()

    for other in (2, 1, 3, 0):
        for way in (0, 1):
            free = 1 if other in (0, 1) else 0
            joining(way, free, other).start()
    for other in (2, 1, 3, 0):
        for way in (0, 1):
            busy = 0 if other in (0, 1) else 1
            passing(way, other).wait_recv()
            at = term(way, (1, 3)[busy], other)
            at[...] = (at[...].astype(jnp.float32) + pass_in[way, other].astype(jnp.float32)).astype(
                jnp.bfloat16
            )
            joining(way, busy, other).start()
    for other in (2, 1, 3, 0):
        for way in (0, 1):
            for side in (0, 1):
                joining(way, side, other).wait_recv()
            halves[way, other] = (
                term(way, 0, other)[...].astype(jnp.float32)
                + join_in[way, 0, other].astype(jnp.float32)
                + join_in[way, 1, other].astype(jnp.float32)
            ).astype(jnp.bfloat16)
            if other == 2:
                for side in (0, 1):
                    hop(way, side).start()
            if other in (1, 3):
                side = 0 if other == 1 else 1
                hop(way, side).wait_recv()
                rows = pl.ds(side * quarter, quarter)
                halves[way, other, rows, :] = (
                    halves[way, other, rows, :].astype(jnp.float32)
                    + hop_in[way, side].astype(jnp.float32)
                ).astype(jnp.bfloat16)
                ending(way, side).start()
    for way in (0, 1):
        for side in (0, 1):
            ending(way, side).wait_recv()
        rows = pl.ds(way * half, half)
        value = (
            halves[way, 0].astype(jnp.float32)
            + end_in[way, 0].astype(jnp.float32)
            + end_in[way, 1].astype(jnp.float32)
        )
        kept = (residual[rows, :].astype(jnp.float32) + value).astype(jnp.bfloat16)
        hidden[rows, :] = kept
        wide = kept.astype(jnp.float32)
        scale = lax.rsqrt(jnp.mean(wide * wide, axis=-1, keepdims=True) + epsilon)
        normed[rows, :] = (wide * scale * gain[...]).astype(jnp.bfloat16)
    for way in (0, 1):
        for other in range(4):
            passing(way, other).wait_send()
            for side in (0, 1):
                joining(way, side, other).wait_send()
        for side in (0, 1):
            hop(way, side).wait_send()
            ending(way, side).wait_send()


def project_rows(Y, Z, attended, weight, residual, gain):
    R, width = residual.shape
    half = R // 2
    vmem = pl.BlockSpec(memory_space=pltpu.VMEM)
    dma = pltpu.SemaphoreType.DMA
    shape = jax.ShapeDtypeStruct((R, width), jnp.bfloat16)
    bf16 = jnp.bfloat16
    return pl.pallas_call(
        functools.partial(reduce_kernel, Y, Z),
        out_shape=(shape, shape),
        in_specs=[vmem] * 4,
        out_specs=(vmem, vmem),
        scratch_shapes=[
            pltpu.VMEM((Y * Z, R, width), bf16),
            pltpu.VMEM((2, 4, half, width), bf16),
            pltpu.VMEM((2, 2, 4, half, width), bf16),
            pltpu.VMEM((2, 4, half, width), bf16),
            pltpu.VMEM((2, 2, half // 2, width), bf16),
            pltpu.VMEM((2, 2, half, width), bf16),
            dma((2, 4)), dma((2, 4)), dma((2, 2, 4)), dma((2, 2, 4)),
            dma((2, 2)), dma((2, 2)), dma((2, 2)), dma((2, 2)),
        ],
        compiler_params=pltpu.CompilerParams(
            collective_id=2, has_side_effects=True, vmem_limit_bytes=48 * 1024 * 1024
        ),
        name="project_rows",
    )(attended, weight, residual, gain)


def local(
    layer_input,
    attn_gain,
    query_weight,
    keyval_weight,
    output_weight,
    cache_entries,
    cache_length,
    expert_gain,
    router_weight,
    expert_choice,
    gate_weight,
    up_weight,
    down_weight,
):
    tp_count = lax.axis_size("tp")
    tp_rank = lax.axis_index("tp")
    grp_count = lax.axis_size("grp")
    heads_here = query_weight.shape[1] // HD
    per_group = QH // KVH
    shared_head = tp_rank * heads_here // per_group
    key_columns = lax.dynamic_slice_in_dim(keyval_weight, shared_head * HD, HD, 1)
    value_columns = lax.dynamic_slice_in_dim(keyval_weight, KVH * HD + shared_head * HD, HD, 1)
    joined = jnp.concatenate([query_weight, key_columns, value_columns], axis=1)
    across = grp_count * tp_count // router_weight.shape[1]
    gathered = gather_rows(tp_count // across, across, rms_scale(layer_input, attn_gain))
    projected = jnp.dot(
        gathered.reshape(-1, layer_input.shape[1]), joined, preferred_element_type=jnp.float32
    )
    rows_total = projected.shape[0]
    query_width = heads_here * HD
    length = cache_length[0]
    positions = (length + jnp.arange(rows_total, dtype=jnp.int32)).astype(jnp.float32)
    queries = rotate(
        projected[:, :query_width].reshape(rows_total, heads_here, HD), positions
    ).astype(jnp.bfloat16)
    new_keys = rotate(projected[:, query_width : query_width + HD][:, None, :], positions)[
        :, 0, :
    ].astype(jnp.bfloat16)
    new_values = projected[:, query_width + HD :].astype(jnp.bfloat16)
    initial_state = (
        jnp.full((rows_total, heads_here), mask_floor, jnp.float32),
        jnp.zeros((rows_total, heads_here), jnp.float32),
        jnp.zeros((rows_total, heads_here, HD), jnp.float32),
    )
    causal = (jnp.arange(rows_total)[:, None] >= jnp.arange(rows_total)[None, :])[:, None, :]
    running = attend_block(initial_state, queries, new_keys, new_values, causal)
    splits = tp_count // KVH
    part_index = tp_rank % splits
    own_entries = cache_entries[0, 0]
    running = fetch_keys(running, queries, own_entries, part_index, length)
    attended = (
        (running[2] / running[1][..., None]).astype(jnp.bfloat16).reshape(rows_total, query_width)
    )
    local_rows = layer_input.shape[0]
    hidden_state, normed = project_rows(
        tp_count // across, across, attended, output_weight.T, layer_input, expert_gain[None, :]
    )
    expert_total = router_weight.shape[1]
    top_count = expert_choice.shape[1]
    capacity = max(2, 3 * top_count * local_rows // (2 * expert_total))
    picked = expert_choice[:, :, None] == jnp.arange(expert_total, dtype=jnp.int32)[None, None, :]
    flat_hits = picked.reshape(local_rows * top_count, expert_total).astype(jnp.int32)
    earlier = jnp.cumsum(flat_hits, axis=0) - flat_hits
    slot_index = jnp.sum(earlier * flat_hits, axis=1).reshape(local_rows, top_count)
    target = expert_choice * capacity + slot_index
    return moe(
        hidden_state,
        normed,
        router_weight,
        target,
        gate_weight[0],
        up_weight[0],
        down_weight[0],
        grp_count // 2,
        tp_count // across,
        across,
        capacity,
    )


def solution(mesh):
    placed = (
        P(("grp", "tp"), None),
        P(),
        P(None, "tp"),
        P(),
        P("tp", None),
        P("grp", "tp", None, None),
        P("grp"),
        P(),
        P(),
        P(("grp", "tp"), None),
        P(("grp", "tp"), None, None),
        P(("grp", "tp"), None, None),
        P(("grp", "tp"), None, None),
    )
    return jax.shard_map(
        local, mesh=mesh, in_specs=placed, out_specs=P(("grp", "tp"), None), check_vma=False
    )
```
